32 devices in a mesh: ctx: 4 (over y, x), ch: 8 (over z, core).
Axes of the slice: x: 2, y: 2, z: 4, core: 2. Of those that a mesh axis runs over, the one named last changes fastest.
Arguments:
- queries: bfloat16 [1024, 4096], P('ctx', 'ch')
- keys: bfloat16 [1024, 4096], P('ctx', 'ch')
- values: bfloat16 [1024, 4096], P('ctx', 'ch'), may hold values from -6 to 6
- block_pattern: int32 [8, 8], replicated, may hold values from 0 to 7, as said below
- out_weight: bfloat16 [4096, 8192], P('ch'), may hold values from -0.09375 to 0.09375
- out_cotangent: bfloat16 [1024, 8192], P('ctx', 'ch'), may hold values from -6 to 6
- conv_taps: float32 [7, 4096], P(None, 'ch'), may hold values from -3 to 3
- tap_lengths: int32 [4096], P('ch'), may hold values from 1 to 7
Outputs:
- grad_queries: bfloat16 [1024, 4096], P('ctx', 'ch')
- grad_keys: bfloat16 [1024, 4096], P('ctx', 'ch')
- grad_values: bfloat16 [1024, 4096], P('ctx', 'ch')
The draws below stay inside these ranges and needn't reach their ends.
Inputs may be any that keep to these rules, and one draw needn't show every extreme that they name: `block_pattern`: row b lists b, b - 1, ..., b - 4 + 1 (each raised to 0 where negative) in its first 4 entries; its other entries are multiples of 4 not above max(b - 4, 0); a block may be listed more than once.
All inputs are finite; a program needn't handle non-finite values.
Results may differ from the reference program's by a relative error of at most 0.025.
Values may be sent and summed in bfloat16 or wider, within the bound.
No kernel may reach another device: no remote copies, remote signals or barrier semaphores. Data moves between devices by JAX's collectives and lax.ppermute only.
A program may use at most 64 MiB of HBM per device.

```python
import jax
import jax.numpy as jnp
from jax import lax

D = 8192
H = 32
HD = 128
BLK = 128
NSEL = 8
WIN = 4
STRIDE = 4
LF = 7
SEQ = 1024
NQB = 8


def query_key_pair(key):
    shape = (SEQ, H * HD)
    base_key = jax.random.normal(jax.random.fold_in(key, 101), shape, jnp.float32)
    base_query = jax.random.normal(jax.random.fold_in(key, 102), shape, jnp.float32)
    return (base_query, base_key)


def draw_queries(key, part):
    return query_key_pair(key)[0].astype(jnp.bfloat16)


def draw_keys(key, part):
    return query_key_pair(key)[1].astype(jnp.bfloat16)


def draw_block_pattern(key, part):
    rows = jnp.arange(NQB, dtype=jnp.int32)[:, None]
    slots = jnp.arange(NSEL, dtype=jnp.int32)[None, :]
    local_part = jnp.maximum(rows - slots, 0)
    raw = jax.random.randint(jax.random.fold_in(key, 7), (NQB, NSEL), 0, 1 << 20, dtype=jnp.int32)
    options = jnp.maximum((rows - WIN + STRIDE) // STRIDE, 1)
    strided = raw % options * STRIDE
    return jnp.where(slots < WIN, local_part, strided).astype(jnp.int32)


def set_ends(array, rng, low, high):
    extent = array.shape
    place = [jax.random.randint(jax.random.fold_in(rng, axis), (), 0, extent[axis]) for axis in range(len(extent))]
    array = array.at[tuple(place)].set(low)
    longest = extent.index(max(extent))
    place[longest] = (place[longest] + 1) % extent[longest]
    return array.at[tuple(place)].set(high)


def levels(rng, extent, cuts, low, largest):
    loudness, own = 1.0, jax.random.fold_in(rng, 6)
    for dim, shards_of in cuts:
        draws = jnp.exp(jax.random.uniform(jax.random.fold_in(own, dim), (shards_of,), jnp.float32, low / len(cuts), largest / len(cuts)))
        loudness = loudness * jnp.repeat(draws, extent[dim] // shards_of).reshape([-1 if axis == dim else 1 for axis in range(len(extent))])
    return loudness


def scatter_about(own_key, extent, scale, most, cuts=(), kind=jnp.bfloat16):
    level = levels(own_key, extent, cuts, -0.22, 0.18) if cuts else 1.0
    drawn = jax.random.normal(own_key, extent, jnp.float32) * scale * level
    return jnp.minimum(jnp.maximum(drawn, -most), most).astype(kind)


def setup_inputs(seed: int = 0) -> dict:
    arg_keys = jax.random.split(jax.random.key(seed), 9)
    queries = draw_queries(jax.random.fold_in(arg_keys[8], 71), 0)
    keys = draw_keys(jax.random.fold_in(arg_keys[8], 71), 0)
    values = scatter_about(arg_keys[2], (SEQ, H * HD), 1.0, 6.0, ((0, 4), (1, 8)))
    block_pattern = draw_block_pattern(jax.random.fold_in(arg_keys[8], 71), 0)
    out_weight = scatter_about(arg_keys[4], (H * HD, D), (H * HD) ** -0.5, 0.09375, ((0, 8),))
    out_cotangent = scatter_about(arg_keys[5], (SEQ, D), 1.0, 6.0, ((0, 4), (1, 8)))
    conv_taps = scatter_about(arg_keys[6], (LF, H * HD), 0.5, 3.0, ((1, 8),), jnp.float32)
    tap_lengths = set_ends(jax.random.randint(arg_keys[7], (H * HD,), 1, LF + 1), jax.random.fold_in(arg_keys[7], 1), 1, LF).astype(jnp.int32)
    return dict(queries=queries, keys=keys, values=values, block_pattern=block_pattern, out_weight=out_weight, out_cotangent=out_cotangent, conv_taps=conv_taps, tap_lengths=tap_lengths)


def allowed_pairs(block_pattern):
    blocks = jnp.arange(NQB, dtype=jnp.int32)
    member = jnp.any(block_pattern[:, :, None] == blocks[None, None, :], axis=1)
    spread = jnp.repeat(jnp.repeat(member, BLK, axis=0), BLK, axis=1)
    places = jnp.arange(SEQ, dtype=jnp.int32)
    return spread & (places[None, :] <= places[:, None])


def head_probs(query_head, key_head, allowed):
    scale = HD ** -0.5
    scores = jnp.dot(query_head, key_head.T, preferred_element_type=jnp.float32) * scale
    masked = jnp.where(allowed, scores, -1e30)
    top = jnp.max(masked, axis=1, keepdims=True)
    total = jnp.sum(jnp.exp(masked - top), axis=1, keepdims=True)
    log_total = top + jnp.log(total)
    return jnp.exp(jnp.where(allowed, scores - log_total, -1e30))


def split_heads(field):
    return field.reshape(SEQ, H, HD).transpose(1, 0, 2)


def join_heads(field):
    return field.transpose(1, 0, 2).reshape(SEQ, H * HD)


def reference(queries, keys, values, block_pattern, out_weight, out_cotangent, conv_taps, tap_lengths):
    allowed = allowed_pairs(block_pattern)
    query_heads = split_heads(queries)
    key_heads = split_heads(keys)
    value_heads = split_heads(values)

    def forward_one(parts):
        query_head, key_head, value_head = parts
        probs = head_probs(query_head, key_head, allowed)
        return jnp.dot(probs.astype(jnp.bfloat16), value_head, preferred_element_type=jnp.float32).astype(jnp.bfloat16)

    attended = lax.map(forward_one, (query_heads, key_heads, value_heads))
    grad_mixed = jnp.dot(out_cotangent, out_weight.T, preferred_element_type=jnp.float32).astype(jnp.bfloat16)
    padded = jnp.concatenate([grad_mixed.astype(jnp.float32), jnp.zeros((LF - 1, H * HD), jnp.float32)], axis=0)
    grad_attn = jnp.zeros((SEQ, H * HD), jnp.float32)
    for shift_tap in range(LF):
        weights_now = jnp.where(tap_lengths > shift_tap, conv_taps[shift_tap], 0.0)
        grad_attn = grad_attn + weights_now[None, :] * padded[shift_tap:shift_tap + SEQ]
    grad_attn = grad_attn.astype(jnp.bfloat16)
    grad_heads = split_heads(grad_attn)

    def backward_one(parts):
        query_head, key_head, value_head, attended_head, grad_head = parts
        scale = HD ** -0.5
        probs = head_probs(query_head, key_head, allowed)
        inner = jnp.sum(grad_head.astype(jnp.float32) * attended_head.astype(jnp.float32), axis=1, keepdims=True)
        grad_probs = jnp.dot(grad_head, value_head.T, preferred_element_type=jnp.float32)
        grad_scores = (probs * (grad_probs - inner)).astype(jnp.bfloat16)
        grad_query = (jnp.dot(grad_scores, key_head, preferred_element_type=jnp.float32) * scale).astype(jnp.bfloat16)
        grad_key = (jnp.dot(grad_scores.T, query_head, preferred_element_type=jnp.float32) * scale).astype(jnp.bfloat16)
        grad_value = jnp.dot(probs.astype(jnp.bfloat16).T, grad_head, preferred_element_type=jnp.float32).astype(jnp.bfloat16)
        return grad_query, grad_key, grad_value

    grad_q, grad_k, grad_v = lax.map(backward_one, (query_heads, key_heads, value_heads, attended, grad_heads))
    return join_heads(grad_q), join_heads(grad_k), join_heads(grad_v)
```

```python
import jax
import jax.numpy as jnp
from jax import lax
from jax.experimental import pallas as pl
from jax.experimental.pallas import tpu as pltpu
from jax.sharding import PartitionSpec as P

HD = 128
BLK = 128
NSEL = 8
WIN = 4
STRIDE = 4
LF = 7


VMEM_SPEC = pl.BlockSpec(memory_space=pltpu.VMEM)
SMEM_SPEC = pl.BlockSpec(memory_space=pltpu.SMEM)


def listed_blocks(block):
    return sorted({0} | {max(block - back, 0) for back in range(WIN)})


def key_runs(block):
    runs = []
    for e in listed_blocks(block):
        if runs and runs[-1][0] + runs[-1][1] == e:
            runs[-1][1] += 1
        else:
            runs.append([e, 1])
    return runs


def dot(a, b, dims):
    return lax.dot_general(a, b, (dims, ((), ())), preferred_element_type=jnp.float32)


def probs_kernel(place_ref, *refs):
    count = len(refs) - 5
    pieces, (q_ref, k_ref, kt_ref, v_ref, pt_ref) = refs[:count], refs[count:]
    place = place_ref[0]
    rows = pieces[0].shape[1]
    for r in range(count):
        here = pl.ds((place ^ r) * rows, rows)
        q_ref[here, :] = pieces[r][0]
        k_ref[here, :] = pieces[r][1]
        v_ref[here, :] = pieces[r][2]
    blocks = q_ref.shape[0] // BLK
    for e in range(blocks):
        kt_ref[:, e * BLK : (e + 1) * BLK] = (
            k_ref[e * BLK : (e + 1) * BLK, :].astype(jnp.float32).T.astype(jnp.bfloat16)
        )
    keep = lax.broadcasted_iota(jnp.int32, (BLK, BLK), 0) <= lax.broadcasted_iota(
        jnp.int32, (BLK, BLK), 1
    )
    base = 0
    for b in range(blocks):
        q = q_ref[b * BLK : (b + 1) * BLK, :]
        scores = []
        for e in listed_blocks(b):
            s = dot(k_ref[e * BLK : (e + 1) * BLK, :], q, ((1,), (1,))) * (HD**-0.5)
            scores.append(jnp.where(keep, s, -1e30) if e == b else s)
        top = scores[0]
        for s in scores[1:]:
            top = jnp.maximum(top, s)
        top = jnp.max(top, axis=0, keepdims=True)
        weights = [jnp.exp(s - top) for s in scores]
        total = weights[0]
        for w in weights[1:]:
            total = total + w
        share = 1.0 / jnp.sum(total, axis=0, keepdims=True)
        for w in weights:
            pt_ref[base : base + BLK, :] = (w * share).astype(jnp.bfloat16)
            base += BLK


def grads_kernel(place_ref, *refs, parts, chunks):
    gm = refs[: parts * chunks]
    taps_ref, lens_ref, q_ref, kt_ref, v_ref, pt_ref = refs[parts * chunks : parts * chunks + 6]
    outs = refs[parts * chunks + 6 : parts * chunks + 6 + parts]
    wide, dq, dk, dv = refs[parts * chunks + 6 + parts :]
    place = place_ref[0]
    seq = q_ref.shape[0]
    rows = seq // parts
    piece = rows // chunks
    for r in range(parts):
        for i in range(chunks):
            at = pl.multiple_of((place ^ r) * rows + i * piece, piece)
            wide[pl.ds(at, piece), :] = gm[r * chunks + i][...].astype(jnp.float32)
    wide[seq : seq + 8, :] = jnp.zeros((8, HD), jnp.float32)
    lanes = pl.ds(pl.multiple_of(place * HD, HD), HD)
    lens = lens_ref[:, lanes]
    taps = [
        jnp.where(lens > j, taps_ref[j : j + 1, lanes], 0.0) for j in range(LF)
    ]
    dk[...] = jnp.zeros((seq, HD), jnp.float32)
    dv[...] = jnp.zeros((seq, HD), jnp.float32)
    scale = HD**-0.5
    base = 0
    for b in range(seq // BLK):
        grad = jnp.zeros((BLK, HD), jnp.float32)
        for j in range(LF):
            grad = grad + taps[j] * wide[b * BLK + j : b * BLK + j + BLK, :]
        grad = grad.astype(jnp.bfloat16)
        q = q_ref[b * BLK : (b + 1) * BLK, :]
        probs, grad_probs = [], []
        inner = jnp.zeros((1, BLK), jnp.float32)
        for first, count in key_runs(b):
            keys = slice(first * BLK, (first + count) * BLK)
            pt = pt_ref[base : base + count * BLK, :]
            base += count * BLK
            dv[keys, :] += dot(pt, grad, ((1,), (0,)))
            gp = dot(v_ref[keys, :], grad, ((1,), (1,)))
            pf = pt.astype(jnp.float32)
            inner = inner + jnp.sum(pf * gp, axis=0, keepdims=True)
            probs.append(pf)
            grad_probs.append(gp)
        dqt = jnp.zeros((HD, BLK), jnp.float32)
        for (first, count), pf, gp in zip(key_runs(b), probs, grad_probs):
            keys = slice(first * BLK, (first + count) * BLK)
            ds = (pf * (gp - inner)).astype(jnp.bfloat16)
            dk[keys, :] += dot(ds, q, ((1,), (0,)))
            dqt = dqt + dot(kt_ref[:, keys], ds, ((1,), (0,)))
        dq[b * BLK : (b + 1) * BLK, :] = dqt.T * scale
    for r in range(parts):
        here = pl.ds(pl.multiple_of((place ^ r) * rows, rows), rows)
        outs[r][0] = dq[here, :].astype(jnp.bfloat16)
        outs[r][1] = (dk[here, :] * scale).astype(jnp.bfloat16)
        outs[r][2] = dv[here, :].astype(jnp.bfloat16)


def join_kernel(place_ref, *refs):
    parts = len(refs) - 3
    place = place_ref[0]
    for r in range(parts):
        lanes = pl.ds(pl.multiple_of((place ^ r) * HD, HD), HD)
        for i in range(3):
            refs[parts + i][:, lanes] = refs[r][i]


def call(kernel, outs, scratch=(), inputs=1, name=None):
    return pl.pallas_call(
        kernel,
        out_shape=outs,
        in_specs=[SMEM_SPEC] + [VMEM_SPEC] * inputs,
        out_specs=[VMEM_SPEC] * len(outs),
        scratch_shapes=list(scratch),
        name=name,
    )


def swap(value, axis, r):
    count = lax.axis_size(axis)
    return lax.ppermute(value, axis, [(i, i ^ r) for i in range(count)])


def projected(cotangent, out_weight):
    count = lax.axis_size("ch")
    line = count // 2
    place = lax.axis_index("ch")
    spot, core = place // 2, place % 2
    cols = cotangent.shape[1]
    chunks = cotangent.shape[0] // BLK

    def part(value, source):
        other = swap(value, "ch", 1)
        total = 0.0
        for shard, k in ((value, core), (other, 1 - core)):
            w = lax.dynamic_slice_in_dim(out_weight, (2 * source + k) * cols, cols, 1)
            total = total + dot(shard, w, ((1,), (1,)))
        return total

    def up(i):
        return [(h, h + 2) for h in range(2 * (i - 1), count - 2)]

    def down(i):
        return [(h, h - 2) for h in range(2, count - 2 * (i - 1))]

    result = []
    shards = [cotangent[i * BLK : (i + 1) * BLK] for i in range(chunks)]
    totals = [0.0] * chunks
    ups, downs = list(shards), list(shards)
    for step in range(1, line):
        if 2 * step > line + 1:
            moved = [lax.ppermute(v, "ch", up(step) + down(step)) for v in ups]
            ups = downs = moved
        else:
            new_ups, new_downs = [], []
            for u, d in zip(ups, downs):
                new_ups.append(lax.ppermute(u, "ch", up(step)))
                new_downs.append(lax.ppermute(d, "ch", down(step)))
            ups, downs = new_ups, new_downs
        if step == 1:
            totals = [t + part(v, spot) for t, v in zip(totals, shards)]
        below, above = jnp.maximum(spot - step, 0), jnp.minimum(spot + step, line - 1)
        if 2 * step >= line:
            ups = downs = [
                u if u is d else jnp.where(spot >= step, u, d) for u, d in zip(ups, downs)
            ]
            source = jnp.where(spot >= step, below, above)
            totals = [t + part(v, source) for t, v in zip(totals, ups)]
        else:
            totals = [
                t + part(u, below) + part(d, above) for t, u, d in zip(totals, ups, downs)
            ]
    return [t.astype(jnp.bfloat16) for t in totals]


def shards_heads(
    queries, keys, values, block_pattern, out_weight, out_cotangent, conv_taps, tap_lengths
):
    parts = lax.axis_size("ctx")
    place = lax.axis_index("ctx")
    where = place.reshape(1).astype(jnp.int32)
    rows = queries.shape[0]
    seq = rows * parts
    blocks = seq // BLK
    pairs = sum(len(listed_blocks(b)) for b in range(blocks))
    low = jnp.bfloat16

    def head(value, r):
        return lax.dynamic_slice_in_dim(value, (place ^ r) * HD, HD, 1)

    grad_mixed = projected(out_cotangent, out_weight)
    pieces = [jnp.stack([head(v, r) for v in (queries, keys, values)]) for r in range(parts)]
    pieces = [pieces[0]] + [swap(pieces[r], "ctx", r) for r in range(1, parts)]
    q, k, kt, v, pt = call(
        probs_kernel,
        [
            jax.ShapeDtypeStruct((seq, HD), low),
            jax.ShapeDtypeStruct((seq, HD), low),
            jax.ShapeDtypeStruct((HD, seq), low),
            jax.ShapeDtypeStruct((seq, HD), low),
            jax.ShapeDtypeStruct((pairs * BLK, BLK), low),
        ],
        inputs=parts,
        name="probs",
    )(where, *pieces)
    mixed = []
    for r in range(parts):
        for chunk in grad_mixed:
            mixed.append(swap(head(chunk, r), "ctx", r) if r else head(chunk, r))
    grads = call(
        lambda *refs: grads_kernel(*refs, parts=parts, chunks=len(grad_mixed)),
        [jax.ShapeDtypeStruct((3, rows, HD), low)] * parts,
        scratch=[pltpu.VMEM((seq + 8, HD), jnp.float32)] + [pltpu.VMEM((seq, HD), jnp.float32)] * 3,
        inputs=len(mixed) + 6,
        name="grads",
    )(where, *mixed, conv_taps, tap_lengths.reshape(1, -1), q, kt, v, pt)
    grads = [grads[0]] + [swap(grads[r], "ctx", r) for r in range(1, parts)]
    return tuple(
        call(
            join_kernel,
            [jax.ShapeDtypeStruct((rows, parts * HD), low)] * 3,
            inputs=parts,
            name="join",
        )(where, *grads)
    )


def shifted(value, axis, steps):
    count = lax.axis_size(axis)
    leading, last = (max(0, -steps), min(count, count - steps))
    return lax.ppermute(value, axis, [(source, source + steps) for source in range(leading, last)])


def shards_any(queries, keys, values, block_pattern, out_weight, out_cotangent, conv_taps, tap_lengths):
    rows_here = queries.shape[0]
    width_here = queries.shape[1]
    heads_here = width_here // HD
    blocks_here = rows_here // BLK
    ctx_count = lax.axis_size("ctx")
    ctx_place = lax.axis_index("ctx")
    seq_rows = rows_here * ctx_count
    key_blocks = seq_rows // BLK
    scale = HD ** (-0.5)
    grad_mixed = lax.dot_general(
        lax.all_gather(out_cotangent, "ch", axis=1, tiled=True),
        out_weight,
        (((1,), (1,)), ((), ())),
        preferred_element_type=jnp.float32,
    ).astype(jnp.bfloat16)
    following = shifted(grad_mixed[: LF - 1], "ctx", -1)
    extended = jnp.concatenate([grad_mixed, following], axis=0).astype(jnp.float32)
    grad_sum = jnp.zeros((rows_here, width_here), jnp.float32)
    for shift_tap in range(LF):
        weights_now = jnp.where(tap_lengths > shift_tap, conv_taps[shift_tap], 0.0)
        grad_sum = grad_sum + weights_now[None, :] * extended[shift_tap : shift_tap + rows_here]
    grad_attn = grad_sum.astype(jnp.bfloat16)
    all_keys, all_values = (
        lax.all_gather(keys, "ctx", axis=0, tiled=True),
        lax.all_gather(values, "ctx", axis=0, tiled=True),
    )
    chosen = lax.dynamic_slice_in_dim(block_pattern, ctx_place * blocks_here, blocks_here, 0)
    slots = jnp.arange(NSEL)
    repeated = jnp.any(
        (chosen[:, :, None] == chosen[:, None, :]) & (slots[None, None, :] < slots[None, :, None]),
        axis=2,
    )
    picked_keys = all_keys.reshape(key_blocks, BLK, heads_here, HD)[chosen]
    picked_values = all_values.reshape(key_blocks, BLK, heads_here, HD)[chosen]
    query_tiles = queries.reshape(blocks_here, BLK, heads_here, HD)
    grad_tiles = grad_attn.reshape(blocks_here, BLK, heads_here, HD)
    offsets = jnp.arange(BLK)
    query_places = (ctx_place * blocks_here + jnp.arange(blocks_here))[:, None] * BLK + offsets[
        None, :
    ]
    key_places = chosen[:, :, None] * BLK + offsets[None, None, :]
    allowed = (~repeated)[:, None, :, None] & (
        key_places[:, None, :, :] <= query_places[:, :, None, None]
    )
    allowed = allowed[:, None]
    scores = (
        jnp.einsum(
            "bqhd,bjkhd->bhqjk", query_tiles, picked_keys, preferred_element_type=jnp.float32
        )
        * scale
    )
    masked = jnp.where(allowed, scores, -1e30)
    top = jnp.max(masked, axis=(3, 4), keepdims=True)
    total = jnp.sum(jnp.exp(masked - top), axis=(3, 4), keepdims=True)
    log_total = top + jnp.log(total)
    probs = jnp.exp(jnp.where(allowed, scores - log_total, -1e30))
    probs_low = probs.astype(jnp.bfloat16)
    attended = jnp.einsum(
        "bhqjk,bjkhd->bqhd", probs_low, picked_values, preferred_element_type=jnp.float32
    ).astype(jnp.bfloat16)
    inner = jnp.sum(grad_tiles.astype(jnp.float32) * attended.astype(jnp.float32), axis=3)
    inner_wide = inner.transpose(0, 2, 1)[:, :, :, None, None]
    grad_probs = jnp.einsum(
        "bqhd,bjkhd->bhqjk", grad_tiles, picked_values, preferred_element_type=jnp.float32
    )
    grad_scores = (probs * (grad_probs - inner_wide)).astype(jnp.bfloat16)
    grad_query = (
        jnp.einsum(
            "bhqjk,bjkhd->bqhd", grad_scores, picked_keys, preferred_element_type=jnp.float32
        )
        * scale
    ).astype(jnp.bfloat16)
    grad_query = grad_query.reshape(rows_here, width_here)
    key_term = (
        jnp.einsum(
            "bhqjk,bqhd->bjkhd", grad_scores, query_tiles, preferred_element_type=jnp.float32
        )
        * scale
    )
    value_term = jnp.einsum(
        "bhqjk,bqhd->bjkhd", probs_low, grad_tiles, preferred_element_type=jnp.float32
    )
    both_terms = jnp.concatenate(
        [
            key_term.reshape(blocks_here, NSEL, BLK, width_here),
            value_term.reshape(blocks_here, NSEL, BLK, width_here),
        ],
        axis=-1,
    )
    block_hot = (chosen[:, :, None] == jnp.arange(key_blocks)[None, None, :]).astype(jnp.float32)
    placed = jnp.einsum(
        "bjn,bjkc->nkc", block_hot, both_terms, precision=lax.Precision.HIGHEST
    ).reshape(seq_rows, 2 * width_here)
    summed = lax.psum_scatter(placed, "ctx", scatter_dimension=0, tiled=True)
    key_sum = summed[:, :width_here]
    value_sum = summed[:, width_here:]
    return (grad_query, key_sum.astype(jnp.bfloat16), value_sum.astype(jnp.bfloat16))


def shards(queries, *others):
    parts = lax.axis_size("ctx")
    heads = queries.shape[1] // HD
    blocks = queries.shape[0] * parts // BLK
    single = blocks - 1 - WIN < STRIDE
    paired = lax.axis_size("ch") % 2 == 0 and parts & (parts - 1) == 0
    if single and paired and heads == parts and queries.shape[0] % BLK == 0:
        return shards_heads(queries, *others)
    return shards_any(queries, *others)


def solution(mesh):
    return jax.shard_map(
        shards,
        mesh=mesh,
        in_specs=(
            P("ctx", "ch"),
            P("ctx", "ch"),
            P("ctx", "ch"),
            P(),
            P("ch", None),
            P("ctx", "ch"),
            P(None, "ch"),
            P("ch"),
        ),
        out_specs=(P("ctx", "ch"), P("ctx", "ch"), P("ctx", "ch")),
        check_vma=False,
    )
```
